512 devices in a mesh: ctx: 64 (over x, y, core), heads: 8 (over z).
Axes of the slice: x: 4, y: 8, z: 8, core: 2. Of those that a mesh axis runs over, the one named last changes fastest.
Arguments:
- ssm_input: bfloat16 [12288, 8192], P('ctx', 'heads'), may hold values from -36 to 36
- gate_input: bfloat16 [12288, 8192], P('ctx', 'heads'), may hold values from -6 to 6
- write_proj: bfloat16 [12288, 128], P('ctx'), may hold values from -0.5 to 0.5
- read_proj: bfloat16 [12288, 128], P('ctx'), may hold values from -0.5 to 0.5
- log_decay: float32 [12288, 128], P('ctx', 'heads'), may hold values from -0.75 to 0, as said below
- skip_gain: float32 [128], P('heads'), may hold values from 0.5 to 2
- norm_gain: float32 [8192], P('heads'), may hold values from 0.1 to 1.9
- query_rows: bfloat16 [12288, 4096], P('ctx', 'heads'), may hold values from -6 to 6
- key_rows: bfloat16 [12288, 1024], P('ctx', 'heads'), may hold values from -6 to 6
- value_rows: bfloat16 [12288, 1024], P('ctx', 'heads'), may hold values from -6 to 6
Outputs:
- ssm_out: bfloat16 [12288, 8192], P('ctx', 'heads')
- attn_out: bfloat16 [12288, 4096], P('ctx', 'heads')
The draws below stay inside these ranges and needn't reach their ends.
Inputs may be any that keep to these rules, and one draw needn't show every extreme that they name: `log_decay`: negative everywhere.
All inputs are finite; a program needn't handle non-finite values.
Results may differ from the reference program's by a relative error of at most 0.0075.
Values may be sent and summed in bfloat16 or wider, within the bound.
No kernel may reach another device: no remote copies, remote signals or barrier semaphores. Data moves between devices by JAX's collectives and lax.ppermute only.
A program may use at most 128 MiB of HBM per device.

```python
import math
import jax
import jax.numpy as jnp
from jax import lax

SSM_HEADS = 128
HEAD_P = 64
STATE = 128
QUERY_HEADS = 32
KV_HEADS = 8
HEAD_DIM = 128
SPAN = 64
TOK_DEV = 192
SEQUENCE_TOKENS = 12288


def draw_ssm_input(key, part):
    split_random_keys = jax.random.split(key, 3)
    width_all = SSM_HEADS * HEAD_P
    basis = jnp.clip(jax.random.normal(split_random_keys[0], (SEQUENCE_TOKENS, width_all), jnp.float32), -3.0, 3.0)
    head_place = (jnp.arange(width_all) // HEAD_P).astype(jnp.float32) / max(SSM_HEADS - 1, 1)
    column_scale = jnp.exp(jax.random.uniform(split_random_keys[1], (width_all,), jnp.float32, math.log(0.25), math.log(2.5)))
    column_scale = column_scale * (1.0 + head_place)
    row_scale = jnp.exp(jax.random.uniform(split_random_keys[2], (SEQUENCE_TOKENS, 1), jnp.float32, math.log(0.5), math.log(1.6)))
    return (basis * column_scale[None, :] * row_scale).astype(jnp.bfloat16)


def draw_log_decay(key, part):
    split_random_keys = jax.random.split(key, 7)
    keep_share = 0.5
    slow_heads = jax.random.uniform(split_random_keys[0], (SSM_HEADS,), jnp.float32) < keep_share
    slow_rate = jnp.exp(jax.random.uniform(split_random_keys[1], (SSM_HEADS,), jnp.float32, math.log(0.15), math.log(0.6))) / SEQUENCE_TOKENS
    fast_rate = jnp.exp(jax.random.uniform(split_random_keys[2], (SSM_HEADS,), jnp.float32, math.log(0.04), math.log(0.07)))
    per_head_rate = jnp.where(slow_heads, slow_rate, fast_rate)
    block_count = SEQUENCE_TOKENS // TOK_DEV
    block_factor = jnp.exp(jax.random.uniform(split_random_keys[3], (block_count,), jnp.float32, math.log(0.5), math.log(2.0)))
    row_index_list = jnp.arange(SEQUENCE_TOKENS)
    row_multiplier = block_factor[row_index_list // TOK_DEV]
    jaggedness_measure = jax.random.uniform(split_random_keys[4], (SEQUENCE_TOKENS, SSM_HEADS), jnp.float32, 0.5, 1.5)
    spike_row_values = jax.random.randint(split_random_keys[5], (3,), 0, SEQUENCE_TOKENS)
    spike_penalty = jax.random.uniform(split_random_keys[6], (3,), jnp.float32, 0.22, 0.5)
    spike_sum_total = jnp.sum(jnp.where(row_index_list[:, None] == spike_row_values[None, :], spike_penalty[None, :], 0.0), axis=1)
    return -(per_head_rate[None, :] * row_multiplier[:, None] * jaggedness_measure) - spike_sum_total[:, None]


def drawn_rows(key, width_all):
    return jnp.clip(jax.random.normal(key, (SEQUENCE_TOKENS, width_all), jnp.float32), -6.0, 6.0)


def draw_query_rows(key, part):
    basis = drawn_rows(jax.random.fold_in(key, 1), QUERY_HEADS * HEAD_DIM)
    return basis.astype(jnp.bfloat16)


def draw_key_rows(key, part):
    basis = drawn_rows(jax.random.fold_in(key, 2), KV_HEADS * HEAD_DIM)
    return basis.astype(jnp.bfloat16)


def shard_levels(stream_key, extent, cuts, smallest, top_value):
    def one(axis_at, parts):
        steps = jax.random.uniform(jax.random.fold_in(jax.random.fold_in(stream_key, 6), axis_at), (parts,), jnp.float32, smallest / len(cuts), top_value / len(cuts))
        return jnp.repeat(jnp.exp(steps), extent[axis_at] // parts).reshape((-1,) + (1,) * (len(extent) - axis_at - 1))

    factor_of = one(*cuts[0])
    for cut in cuts[1:]:
        factor_of = factor_of * one(*cut)
    return factor_of


def gaussian(stream_key, dims, deviation, bound, cuts=(), held_as=jnp.bfloat16):
    factor_of = shard_levels(stream_key, dims, cuts, -0.22, 0.18) if cuts else 1.0
    values = jax.random.normal(stream_key, dims, jnp.float32) * deviation * factor_of
    return jnp.minimum(jnp.maximum(values, -bound), bound).astype(held_as)


def setup_inputs(seed: int = 0) -> dict:
    arg_keys = jax.random.split(jax.random.key(seed), 11)
    return {
        "ssm_input": draw_ssm_input(jax.random.fold_in(arg_keys[10], 71), 0),
        "gate_input": gaussian(arg_keys[1], (SEQUENCE_TOKENS, SSM_HEADS * HEAD_P), 1.0, 6.0, ((0, 64), (1, 8))),
        "write_proj": gaussian(arg_keys[2], (SEQUENCE_TOKENS, STATE), STATE ** -0.5, 0.5, ((0, 64),)),
        "read_proj": gaussian(arg_keys[3], (SEQUENCE_TOKENS, STATE), STATE ** -0.5, 0.5, ((0, 64),)),
        "log_decay": draw_log_decay(jax.random.fold_in(arg_keys[10], 71), 0),
        "skip_gain": jnp.clip(0.5 + 1.5 * jax.random.uniform(arg_keys[5], (SSM_HEADS,), jnp.float32) ** shard_levels(arg_keys[5], (SSM_HEADS,), ((0, 8),), -0.2, 0.2), 0.5, 2.0),
        "norm_gain": jnp.clip(1.0 + 0.18 * jax.random.normal(arg_keys[6], (SSM_HEADS * HEAD_P,), jnp.float32), 0.1, 1.9),
        "query_rows": draw_query_rows(jax.random.fold_in(arg_keys[10], 71), 0),
        "key_rows": draw_key_rows(jax.random.fold_in(arg_keys[10], 71), 0),
        "value_rows": gaussian(arg_keys[9], (SEQUENCE_TOKENS, KV_HEADS * HEAD_DIM), 1.0, 6.0, ((0, 64), (1, 8))),
    }


def state_mixer(ssm_input, gate_input, write_proj, read_proj, log_decay, skip_gain, norm_gain):
    block_count = SEQUENCE_TOKENS // SPAN
    inputs_blk = ssm_input.reshape(block_count, SPAN, SSM_HEADS, HEAD_P)
    write_blk = write_proj.reshape(block_count, SPAN, STATE)
    read_blk = read_proj.reshape(block_count, SPAN, STATE)
    decay_blk = log_decay.reshape(block_count, SPAN, SSM_HEADS)
    causal = jnp.arange(SPAN)[:, None] >= jnp.arange(SPAN)[None, :]

    def span_step(state_in, block_item):
        x_block, write_block, read_block, decay_block = block_item
        cum_decay = jnp.cumsum(decay_block, axis=0)
        cum_heads = cum_decay.T
        decay_gap = cum_heads[:, :, None] - cum_heads[:, None, :]
        decay_mask = jnp.where(causal[None], jnp.exp(jnp.where(causal[None], decay_gap, 0.0)), 0.0)
        intersection = jnp.dot(read_block, write_block.T, preferred_element_type=jnp.float32)
        mix_weights = intersection[None] * decay_mask
        x_float = x_block.astype(jnp.float32)
        y_local = jnp.einsum('hts,shp->thp', mix_weights, x_float, precision=lax.Precision.HIGHEST)
        tail_decay = jnp.exp(cum_heads[:, -1:] - cum_heads)
        weighted_write = tail_decay[:, :, None] * write_block.astype(jnp.float32)[None]
        block_state = jnp.einsum('shp,hsn->hpn', x_float, weighted_write, precision=lax.Precision.HIGHEST)
        y_carry = jnp.einsum('tn,hpn->thp', read_block.astype(jnp.float32), state_in, precision=lax.Precision.HIGHEST) * jnp.exp(cum_decay)[:, :, None]
        mixed_out = y_local + y_carry + skip_gain[None, :, None] * x_float
        state_out = jnp.exp(cum_heads[:, -1])[:, None, None] * state_in + block_state
        return (state_out, mixed_out)
    state_zero = jnp.zeros((SSM_HEADS, HEAD_P, STATE), jnp.float32)
    _, mixed_all = lax.scan(span_step, state_zero, (inputs_blk, write_blk, read_blk, decay_blk))
    mixed_all = mixed_all.reshape(SEQUENCE_TOKENS, SSM_HEADS * HEAD_P)
    gated = mixed_all * jax.nn.silu(gate_input.astype(jnp.float32))
    mean_square = lax.optimization_barrier(jnp.mean(gated * gated, axis=1, keepdims=True))
    return (gated * lax.rsqrt(mean_square + 1e-05) * norm_gain[None, :]).astype(jnp.bfloat16)

def attention(query_rows, key_rows, value_rows):
    group_size = QUERY_HEADS // KV_HEADS
    scale_factor = 1.0 / HEAD_DIM ** 0.5
    queries_all = query_rows.reshape(SEQUENCE_TOKENS, QUERY_HEADS, HEAD_DIM)
    keys_all = key_rows.reshape(SEQUENCE_TOKENS, KV_HEADS, HEAD_DIM)
    values_all = value_rows.reshape(SEQUENCE_TOKENS, KV_HEADS, HEAD_DIM)
    block_total = SEQUENCE_TOKENS // TOK_DEV
    key_positions = jnp.arange(SEQUENCE_TOKENS, dtype=jnp.int32)

    def one_block(flat_index):
        head_index = flat_index // block_total
        block_index = flat_index % block_total
        first_row = (block_index * TOK_DEV).astype(jnp.int32)
        query_block = lax.dynamic_slice_in_dim(queries_all, first_row, TOK_DEV, 0)
        query_block = lax.dynamic_index_in_dim(query_block, head_index, 1, keepdims=False)
        kv_index = (head_index // group_size).astype(jnp.int32)
        key_head = lax.dynamic_index_in_dim(keys_all, kv_index, 1, keepdims=False)
        value_head = lax.dynamic_index_in_dim(values_all, kv_index, 1, keepdims=False)
        scores = jnp.dot(query_block, key_head.T, preferred_element_type=jnp.float32) * scale_factor
        query_positions = first_row + jnp.arange(TOK_DEV, dtype=jnp.int32)
        visible = key_positions[None, :] <= query_positions[:, None]
        row_max = lax.optimization_barrier(jnp.max(jnp.where(visible, scores, -jnp.inf), axis=1, keepdims=True))
        weights = jnp.where(visible, jnp.exp(jnp.where(visible, scores - row_max, 0.0)), 0.0)
        weight_sum = lax.optimization_barrier(jnp.sum(weights, axis=1, keepdims=True))
        result = jnp.dot(weights.astype(jnp.bfloat16), value_head, preferred_element_type=jnp.float32) / weight_sum
        return result.astype(jnp.bfloat16)
    blocks_out = lax.map(one_block, jnp.arange(QUERY_HEADS * block_total, dtype=jnp.int32))
    blocks_out = blocks_out.reshape(QUERY_HEADS, block_total, TOK_DEV, HEAD_DIM)
    return jnp.transpose(blocks_out, (1, 2, 0, 3)).reshape(SEQUENCE_TOKENS, QUERY_HEADS * HEAD_DIM)

def reference(ssm_input, gate_input, write_proj, read_proj, log_decay, skip_gain, norm_gain, query_rows, key_rows, value_rows):
    ssm_out = state_mixer(ssm_input, gate_input, write_proj, read_proj, log_decay, skip_gain, norm_gain)
    attn_out = attention(query_rows, key_rows, value_rows)
    return (ssm_out, attn_out)
```

```python
import functools

import jax
import jax.numpy as jnp
from jax import lax
from jax.experimental import pallas as pl
from jax.experimental.pallas import tpu as pltpu
from jax.sharding import PartitionSpec as P

SSM_HEADS = 128
HEAD_P = 64
STATE = 128
HEAD_DIM = 128
PLACES = 64
LANES = 128
KEYS = 768
HIGH = lax.Precision.HIGHEST
F32 = jnp.float32
BF16 = jnp.bfloat16
VMEM_LIMIT = 48 * 1024 * 1024


def dot(a, b, ca, cb, precision=None):
    return lax.dot_general(
        a, b, (((ca,), (cb,)), ((), ())), precision=precision, preferred_element_type=F32
    )


def head_expansion(heads, width):
    row = lax.broadcasted_iota(jnp.int32, (heads, width), 0)
    col = lax.broadcasted_iota(jnp.int32, (heads, width), 1)
    return (col // HEAD_P == row).astype(F32)


def lower_mask(rows):
    t = lax.broadcasted_iota(jnp.int32, (rows, rows), 0)
    s = lax.broadcasted_iota(jnp.int32, (rows, rows), 1)
    return t >= s


def state_kernel(x_ref, write_ref, decay_ref, out_ref):
    rows, width = x_ref.shape
    heads = decay_ref.shape[1]
    share = width // PLACES
    decay = decay_ref[...]
    later = (~lower_mask(rows)).astype(F32)
    tail = jnp.exp(dot(later, decay, 1, 0, HIGH))
    tail = dot(tail, head_expansion(heads, width), 1, 0, HIGH)
    scaled = (x_ref[...].astype(F32) * tail).astype(BF16)
    state = dot(scaled, write_ref[...], 0, 0)
    out_ref[:, 0:share, :] = state.reshape(PLACES, share, STATE).astype(BF16)
    total = dot(decay, jnp.ones((rows, LANES), F32), 0, 0, HIGH)
    high = total.astype(BF16).astype(F32)
    middle = (total - high).astype(BF16).astype(F32)
    low = (total - high - middle).astype(BF16).astype(F32)
    row = lax.broadcasted_iota(jnp.int32, (heads, 8, LANES), 1)
    pieces = jnp.where(
        row == 0,
        high[:, None, :],
        jnp.where(row == 1, middle[:, None, :], jnp.where(row == 2, low[:, None, :], 0.0)),
    )
    pieces = jnp.broadcast_to(pieces[:, None], (heads, PLACES // heads, 8, LANES))
    out_ref[:, share : share + 8, :] = pieces.reshape(PLACES, 8, LANES).astype(BF16)


def fold_kernel(parts_ref, out_ref):
    places, deep, lanes = parts_ref.shape
    share = deep - 8
    state = jnp.zeros((share, lanes), F32)
    for i in range(places):
        out_ref[i] = state.astype(BF16)
        if i + 1 < places:
            part = parts_ref[i].astype(F32)
            total = part[share : share + 1] + part[share + 1 : share + 2]
            total = total + part[share + 2 : share + 3]
            state = state * jnp.exp(total) + part[0:share]


def mixer_kernel(
    x_ref, gate_ref, write_ref, read_ref, decay_ref, skip_ref, start_ref, gated_ref, square_ref
):
    rows, width = x_ref.shape
    heads = decay_ref.shape[1]
    mask = lower_mask(rows)
    lower = mask.astype(F32)
    decay = decay_ref[...]
    cum = dot(lower, decay, 1, 0, HIGH)
    cum_heads = dot(decay, lower, 0, 1, HIGH)
    expansion = head_expansion(heads, width)
    grown = dot(jnp.exp(cum), expansion, 1, 0, HIGH)
    skip = dot(skip_ref[...], expansion, 1, 0, HIGH)[0:1]
    gain = dot(read_ref[...], write_ref[...], 1, 1)
    carry = dot(read_ref[...], start_ref[...], 1, 1)
    lane = lax.broadcasted_iota(jnp.int32, (rows, LANES), 1)
    total = jnp.zeros((8, rows), F32)
    for pair in range(width // LANES):
        cols = slice(pair * LANES, (pair + 1) * LANES)
        x = x_ref[:, cols]
        found = []
        for h in (2 * pair, 2 * pair + 1):
            gap = cum[:, h : h + 1] - cum_heads[h : h + 1, :]
            mix = gain * jnp.exp(jnp.where(mask, gap, -1e30))
            found.append(dot(mix.astype(BF16), x, 1, 0))
        mixed = jnp.where(lane < HEAD_P, found[0], found[1])
        mixed = mixed + carry[:, cols] * grown[:, cols] + skip[:, cols] * x.astype(F32)
        gate = gate_ref[:, cols].astype(F32)
        gated = mixed * (gate / (1.0 + jnp.exp(-gate)))
        gated_ref[:, cols] = gated
        total = total + dot(jnp.ones((8, LANES), F32), gated * gated, 1, 1, HIGH)
    square_ref[...] = total


def norm_kernel(gated_ref, square_ref, gain_ref, out_ref):
    total = dot(square_ref[...], jnp.ones((square_ref.shape[0], LANES), F32), 0, 0, HIGH)
    scale = lax.rsqrt(total / (SSM_HEADS * HEAD_P) + 1e-05)
    for c in range(0, out_ref.shape[1], LANES):
        cols = slice(c, c + LANES)
        out_ref[:, cols] = (gated_ref[:, cols] * scale * gain_ref[:, cols]).astype(BF16)


def attention_kernel(place_ref, query_ref, kv_ref, out_ref, kv, top, acc, sems):
    rows, width = query_ref.shape
    sets = width // HEAD_DIM
    factor = 1.4426950408889634 / HEAD_DIM**0.5
    place = place_ref[0]
    last = (place * rows) // KEYS

    def fetch(c):
        span = pl.ds(pl.multiple_of(c * KEYS, KEYS), KEYS)
        return pltpu.make_async_copy(kv_ref.at[span], kv.at[span], sems.at[c])

    @pl.loop(0, last + 1)
    def _(c):
        fetch(c).start()

    top[...] = jnp.full(top.shape, -1e30, F32)
    acc[...] = jnp.zeros(acc.shape, F32)

    def step(c, diagonal):
        fetch(c).wait()
        span = pl.ds(pl.multiple_of(c * KEYS, KEYS), KEYS)
        keys = kv[span, 0:HEAD_DIM]
        values = jnp.concatenate(
            [kv[span, HEAD_DIM : 2 * HEAD_DIM], jnp.ones((KEYS, LANES), BF16)], axis=1
        )
        if diagonal:
            t = lax.broadcasted_iota(jnp.int32, (rows, KEYS), 0) + place * rows
            s = lax.broadcasted_iota(jnp.int32, (rows, KEYS), 1) + c * KEYS
            visible = s <= t
        for j in range(sets):
            here = slice(j * rows, (j + 1) * rows)
            scores = dot(query_ref[:, j * HEAD_DIM : (j + 1) * HEAD_DIM], keys, 1, 1)
            if diagonal:
                scores = jnp.where(visible, scores, -1e30)
            old = top[here, 0:1]
            new = jnp.maximum(old, jnp.max(scores, axis=1, keepdims=True))
            weights = jnp.exp2((scores - new) * factor).astype(BF16)
            acc[here] = acc[here] * jnp.exp2((old - new) * factor) + dot(weights, values, 1, 0)
            top[here] = jnp.broadcast_to(new, (rows, LANES))

    @pl.loop(0, last)
    def _(c):
        step(c, False)

    step(last, True)
    for j in range(sets):
        here = slice(j * rows, (j + 1) * rows)
        out_ref[:, j * HEAD_DIM : (j + 1) * HEAD_DIM] = (
            acc[here, 0:HEAD_DIM] / acc[here, HEAD_DIM : 2 * HEAD_DIM]
        ).astype(BF16)


def vmem_call(kernel, outs, name, flops, moved, **more):
    return pl.pallas_call(
        kernel,
        out_shape=outs,
        name=name,
        compiler_params=pltpu.CompilerParams(vmem_limit_bytes=VMEM_LIMIT),
        cost_estimate=pl.CostEstimate(flops=flops, bytes_accessed=moved, transcendentals=0),
        **more,
    )


def body(
    ssm_input,
    gate_input,
    write_proj,
    read_proj,
    log_decay,
    skip_gain,
    norm_gain,
    query_rows,
    key_rows,
    value_rows,
):
    rows, width = ssm_input.shape
    heads = log_decay.shape[1]
    share = width // PLACES
    place = lax.axis_index("ctx").astype(jnp.int32).reshape(1)

    kv = lax.all_gather(
        jnp.concatenate([key_rows, value_rows], axis=1), "ctx", axis=0, tiled=True
    )

    parts = vmem_call(
        state_kernel,
        jax.ShapeDtypeStruct((PLACES, share + 8, STATE), BF16),
        "device_state",
        2 * rows * width * STATE,
        2 * rows * width,
    )(ssm_input, write_proj, log_decay)
    parts = lax.all_to_all(parts, "ctx", 0, 0, tiled=True)
    starts = vmem_call(
        fold_kernel,
        jax.ShapeDtypeStruct((PLACES, share, STATE), BF16),
        "state_fold",
        2 * width * STATE,
        4 * width * STATE,
    )(parts)
    starts = lax.all_to_all(starts, "ctx", 0, 0, tiled=True)
    gated, square = vmem_call(
        mixer_kernel,
        (
            jax.ShapeDtypeStruct((rows, width), F32),
            jax.ShapeDtypeStruct((8, rows), F32),
        ),
        "mixer",
        4 * rows * rows * width,
        12 * rows * width,
    )(
        ssm_input,
        gate_input,
        write_proj,
        read_proj,
        log_decay,
        jnp.broadcast_to(skip_gain[None], (8, heads)),
        starts.reshape(width, STATE),
    )
    square = lax.all_to_all(square, "heads", 0, 0, tiled=True)
    ssm_out = vmem_call(
        norm_kernel,
        jax.ShapeDtypeStruct((rows, width), BF16),
        "norm",
        4 * rows * width,
        6 * rows * width,
    )(gated, square, norm_gain[None])

    length = kv.shape[0]
    attn_out = vmem_call(
        attention_kernel,
        jax.ShapeDtypeStruct(query_rows.shape, BF16),
        "attention",
        2 * rows * 4 * length * 2 * HEAD_DIM,
        2 * length * 2 * HEAD_DIM,
        in_specs=[
            pl.BlockSpec(memory_space=pltpu.SMEM),
            pl.BlockSpec(memory_space=pltpu.VMEM),
            pl.BlockSpec(memory_space=pl.ANY),
        ],
        out_specs=pl.BlockSpec(memory_space=pltpu.VMEM),
        scratch_shapes=[
            pltpu.VMEM((length, 2 * HEAD_DIM), BF16),
            pltpu.VMEM((4 * rows, LANES), F32),
            pltpu.VMEM((4 * rows, 2 * HEAD_DIM), F32),
            pltpu.SemaphoreType.DMA((length // KEYS,)),
        ],
    )(place, query_rows, kv)
    return (ssm_out, attn_out)


def solution(mesh):
    split = P("ctx", "heads")
    in_specs = (
        split,
        split,
        P("ctx", None),
        P("ctx", None),
        split,
        P("heads"),
        P("heads"),
        split,
        split,
        split,
    )
    return jax.shard_map(
        body, mesh=mesh, in_specs=in_specs, out_specs=(split, split), check_vma=False
    )
```

```python
import jax
import jax.numpy as jnp
from jax import lax
from jax.experimental import pallas as pl
from jax.experimental.pallas import tpu as pltpu
from jax.sharding import Mesh
from jax.sharding import PartitionSpec as P

SSM_HEADS = 128
HEAD_P = 64
STATE = 128
HEAD_DIM = 128
PLACES = 64
LANES = 128
GROUP = 16
CTX = ("x", "y", "core")
HIGH = lax.Precision.HIGHEST
F32 = jnp.float32
BF16 = jnp.bfloat16
VMEM_LIMIT = 48 * 1024 * 1024


def dot(a, b, ca, cb, precision=None):
    return lax.dot_general(
        a, b, (((ca,), (cb,)), ((), ())), precision=precision, preferred_element_type=F32
    )


def head_expansion(heads, width):
    row = lax.broadcasted_iota(jnp.int32, (heads, width), 0)
    col = lax.broadcasted_iota(jnp.int32, (heads, width), 1)
    return (col // HEAD_P == row).astype(F32)


def lower_mask(rows):
    t = lax.broadcasted_iota(jnp.int32, (rows, rows), 0)
    s = lax.broadcasted_iota(jnp.int32, (rows, rows), 1)
    return t >= s


def fetch_all(pairs, sems):
    copies = [pltpu.make_async_copy(a, b, sems.at[i]) for i, (a, b) in enumerate(pairs)]
    for copy in copies:
        copy.start()
    return copies


def state_kernel(decay_hbm, x_hbm, write_hbm, out_ref, decay_ref, x_ref, write_ref, sems):
    copies = fetch_all([(decay_hbm, decay_ref), (x_hbm, x_ref), (write_hbm, write_ref)], sems)
    copies[0].wait()
    rows, width = x_ref.shape
    heads = decay_ref.shape[0]
    share = width // PLACES
    decay = decay_ref[...]
    later = (~lower_mask(rows)).astype(F32)
    tail = jnp.exp(dot(later, decay, 1, 1, HIGH))
    tail = dot(tail, head_expansion(heads, width), 1, 0, HIGH)
    total = dot(decay, jnp.ones((rows, LANES), F32), 1, 0, HIGH)
    high = total.astype(BF16).astype(F32)
    middle = (total - high).astype(BF16).astype(F32)
    low = (total - high - middle).astype(BF16).astype(F32)
    row = lax.broadcasted_iota(jnp.int32, (heads, 8, LANES), 1)
    pieces = jnp.where(
        row == 0,
        high[:, None, :],
        jnp.where(row == 1, middle[:, None, :], jnp.where(row == 2, low[:, None, :], 0.0)),
    )
    pieces = jnp.broadcast_to(pieces[:, None], (heads, PLACES // heads, 8, LANES))
    out_ref[:, share : share + 8, :] = pieces.reshape(PLACES, 8, LANES).astype(BF16)
    copies[1].wait()
    copies[2].wait()
    scaled = (x_ref[...].astype(F32) * tail).astype(BF16)
    state = dot(scaled, write_ref[...], 0, 0)
    out_ref[:, 0:share, :] = state.reshape(PLACES, share, STATE).astype(BF16)


def fold_kernel(parts_ref, out_ref):
    places, deep, lanes = parts_ref.shape
    share = deep - 8
    state = jnp.zeros((share, lanes), F32)
    for i in range(places):
        out_ref[i] = state.astype(BF16)
        if i + 1 < places:
            part = parts_ref[i].astype(F32)
            total = part[share : share + 1] + part[share + 1 : share + 2]
            total = total + part[share + 2 : share + 3]
            state = state * jnp.exp(total) + part[0:share]


def mixer_kernel(
    x_hbm,
    gate_hbm,
    write_hbm,
    read_hbm,
    decay_hbm,
    skip_ref,
    start_ref,
    gated_ref,
    square_ref,
    decay_ref,
    x_ref,
    gate_ref,
    write_ref,
    read_ref,
    sems,
):
    copies = fetch_all(
        [
            (decay_hbm, decay_ref),
            (read_hbm, read_ref),
            (write_hbm, write_ref),
            (x_hbm, x_ref),
            (gate_hbm, gate_ref),
        ],
        sems,
    )
    copies[0].wait()
    rows, width = x_ref.shape
    heads = decay_ref.shape[0]
    mask = lower_mask(rows)
    lower = mask.astype(F32)
    decay = decay_ref[...]
    cum = dot(lower, decay, 1, 1, HIGH)
    cum_heads = dot(decay, lower, 1, 1, HIGH)
    expansion = head_expansion(heads, width)
    grown = dot(jnp.exp(cum), expansion, 1, 0, HIGH)
    skip = dot(skip_ref[...], expansion, 1, 0, HIGH)
    copies[1].wait()
    carry = dot(read_ref[...], start_ref[...], 1, 1)
    copies[2].wait()
    gain = dot(read_ref[...], write_ref[...], 1, 1)
    copies[3].wait()
    copies[4].wait()
    lane = lax.broadcasted_iota(jnp.int32, (rows, LANES), 1)
    total = jnp.zeros((8, rows), F32)
    for pair in range(width // LANES):
        cols = slice(pair * LANES, (pair + 1) * LANES)
        x = x_ref[:, cols]
        found = []
        for h in (2 * pair, 2 * pair + 1):
            gap = cum[:, h : h + 1] - cum_heads[h : h + 1, :]
            mix = gain * jnp.exp(jnp.where(mask, gap, -1e30))
            found.append(dot(mix.astype(BF16), x, 1, 0))
        mixed = jnp.where(lane < HEAD_P, found[0], found[1])
        mixed = mixed + carry[:, cols] * grown[:, cols] + skip[:, cols] * x.astype(F32)
        gate = gate_ref[:, cols].astype(F32)
        gated = mixed * (gate / (1.0 + jnp.exp(-gate)))
        gated_ref[:, cols] = gated
        total = total + dot(jnp.ones((8, LANES), F32), gated * gated, 1, 1, HIGH)
    square_ref[...] = total


def norm_kernel(gated_ref, square_ref, gain_ref, out_ref):
    total = dot(square_ref[...], jnp.ones((square_ref.shape[0], LANES), F32), 0, 0, HIGH)
    scale = lax.rsqrt(total / (SSM_HEADS * HEAD_P) + 1e-05)
    for c in range(0, out_ref.shape[1], LANES):
        cols = slice(c, c + LANES)
        out_ref[:, cols] = (gated_ref[:, cols] * scale * gain_ref[:, cols]).astype(BF16)


def attention_kernel(place_ref, query_hbm, kv_ref, out_ref, query_ref, kv, top, acc, sems):
    rows, width = query_ref.shape
    sets = width // HEAD_DIM
    factor = 1.4426950408889634 / HEAD_DIM**0.5
    place = place_ref[0]
    last = place // GROUP
    keys_at_once = GROUP * rows

    def fetch(c):
        first = pl.multiple_of((last - c) * rows, rows)
        return pltpu.make_async_copy(kv_ref.at[:, pl.ds(first, rows)], kv.at[c], sems.at[c])

    copies = fetch_all([(query_hbm, query_ref)], sems.at[pl.ds(sems.shape[0] - 1, 1)])

    @pl.loop(0, last + 1)
    def _(c):
        fetch(c).start()

    top[...] = jnp.full(top.shape, -1e30, F32)
    acc[...] = jnp.zeros(acc.shape, F32)
    copies[0].wait()

    def step(c, diagonal):
        fetch(c).wait()
        block = kv[c].reshape(keys_at_once, 2 * HEAD_DIM)
        keys = block[:, 0:HEAD_DIM]
        values = jnp.concatenate(
            [block[:, HEAD_DIM : 2 * HEAD_DIM], jnp.ones((keys_at_once, LANES), BF16)], axis=1
        )
        if diagonal:
            t = lax.broadcasted_iota(jnp.int32, (rows, keys_at_once), 0) + place * rows
            s = lax.broadcasted_iota(jnp.int32, (rows, keys_at_once), 1) + c * keys_at_once
            visible = s <= t

        def scores_of(j):
            scores = dot(query_ref[:, j * HEAD_DIM : (j + 1) * HEAD_DIM], keys, 1, 1)
            return jnp.where(visible, scores, -1e30) if diagonal else scores

        ahead = scores_of(0)
        for j in range(sets):
            here = slice(j * rows, (j + 1) * rows)
            scores = ahead
            if j + 1 < sets:
                ahead = scores_of(j + 1)
            old = top[here]
            new = jnp.maximum(old, jnp.max(scores, axis=1, keepdims=True))
            weights = jnp.exp2(scores * factor - new[:, 0:1] * factor).astype(BF16)
            shrink = jnp.exp2((old - new) * factor)
            shrink = jnp.concatenate([shrink, shrink], axis=1)
            acc[here] = acc[here] * shrink + dot(weights, values, 1, 0)
            top[here] = new

    @pl.loop(0, last)
    def _(c):
        step(c, False)

    step(last, True)
    for j in range(sets):
        here = slice(j * rows, (j + 1) * rows)
        out_ref[:, j * HEAD_DIM : (j + 1) * HEAD_DIM] = (
            acc[here, 0:HEAD_DIM] / acc[here, HEAD_DIM : 2 * HEAD_DIM]
        ).astype(BF16)


def vmem_call(kernel, outs, name, flops, moved, **more):
    return pl.pallas_call(
        kernel,
        out_shape=outs,
        name=name,
        compiler_params=pltpu.CompilerParams(vmem_limit_bytes=VMEM_LIMIT),
        cost_estimate=pl.CostEstimate(flops=flops, bytes_accessed=moved, transcendentals=0),
        **more,
    )


def body(
    ssm_input,
    gate_input,
    write_proj,
    read_proj,
    log_decay,
    skip_gain,
    norm_gain,
    query_rows,
    key_rows,
    value_rows,
):
    rows, width = ssm_input.shape
    heads = log_decay.shape[1]
    share = width // PLACES
    place = lax.axis_index(CTX).astype(jnp.int32).reshape(1)
    in_vmem = pl.BlockSpec(memory_space=pltpu.VMEM)
    anywhere = pl.BlockSpec(memory_space=pltpu.HBM)
    x_scratch = pltpu.VMEM((rows, width), BF16)
    decay_scratch = pltpu.VMEM((heads, rows), F32)
    side_scratch = pltpu.VMEM((rows, STATE), BF16)

    ssm_input, gate_input, write_proj, read_proj, query_rows, decay = (
        pltpu.with_memory_space_constraint(a, pltpu.HBM)
        for a in (ssm_input, gate_input, write_proj, read_proj, query_rows, log_decay.T)
    )

    own = jnp.concatenate([key_rows, value_rows], axis=1)
    columns = PLACES // GROUP
    held = [own] + [
        lax.ppermute(own, "x", [(i, i + k) for i in range(columns - k)]) for k in range(1, columns)
    ]
    parts = vmem_call(
        state_kernel,
        jax.ShapeDtypeStruct((PLACES, share + 8, STATE), BF16),
        "device_state",
        2 * rows * width * STATE,
        2 * rows * width,
        in_specs=[anywhere] * 3,
        scratch_shapes=[decay_scratch, x_scratch, side_scratch, pltpu.SemaphoreType.DMA((3,))],
    )(decay, ssm_input, write_proj)
    parts, place, *held = lax.optimization_barrier((parts, place, *held))
    kv = lax.all_gather(jnp.concatenate(held, axis=0), ("y", "core"), axis=0)
    parts = lax.all_to_all(parts, CTX, 0, 0, tiled=True)
    starts = vmem_call(
        fold_kernel,
        jax.ShapeDtypeStruct((PLACES, share, STATE), BF16),
        "state_fold",
        2 * width * STATE,
        4 * width * STATE,
    )(parts)
    starts = lax.all_to_all(starts, CTX, 0, 0, tiled=True)
    gated, square = vmem_call(
        mixer_kernel,
        (
            jax.ShapeDtypeStruct((rows, width), F32),
            jax.ShapeDtypeStruct((8, rows), F32),
        ),
        "mixer",
        4 * rows * rows * width,
        12 * rows * width,
        in_specs=[anywhere] * 5 + [in_vmem] * 2,
        scratch_shapes=[decay_scratch]
        + [x_scratch] * 2
        + [side_scratch] * 2
        + [pltpu.SemaphoreType.DMA((5,))],
    )(
        ssm_input,
        gate_input,
        write_proj,
        read_proj,
        decay,
        skip_gain[None],
        starts.reshape(width, STATE),
    )
    square = lax.all_to_all(square, "heads", 0, 0, tiled=True)
    square, query_rows = lax.optimization_barrier((square, query_rows))
    ssm_out = vmem_call(
        norm_kernel,
        jax.ShapeDtypeStruct((rows, width), BF16),
        "norm",
        4 * rows * width,
        6 * rows * width,
    )(gated, square, norm_gain[None])

    attn_out = vmem_call(
        attention_kernel,
        jax.ShapeDtypeStruct(query_rows.shape, BF16),
        "attention",
        2 * rows * 4 * PLACES * rows * 2 * HEAD_DIM,
        2 * PLACES * rows * 2 * HEAD_DIM,
        in_specs=[pl.BlockSpec(memory_space=pltpu.SMEM), anywhere, anywhere],
        scratch_shapes=[
            pltpu.VMEM(query_rows.shape, BF16),
            pltpu.VMEM((columns, GROUP, rows, 2 * HEAD_DIM), BF16),
            pltpu.VMEM((4 * rows, LANES), F32),
            pltpu.VMEM((4 * rows, 2 * HEAD_DIM), F32),
            pltpu.SemaphoreType.DMA((columns + 1,)),
        ],
    )(place, query_rows, kv)
    return (ssm_out, attn_out)


def solution(mesh):
    fine = Mesh(mesh.devices.reshape(4, 8, 2, 8), CTX + ("heads",))
    split = P(CTX, "heads")
    in_specs = (
        split,
        split,
        P(CTX, None),
        P(CTX, None),
        split,
        P("heads"),
        P("heads"),
        split,
        split,
        split,
    )
    return jax.shard_map(
        body, mesh=fine, in_specs=in_specs, out_specs=(split, split), check_vma=False
    )
```

```python
import jax
import jax.numpy as jnp
from jax import lax
from jax.experimental import pallas as pl
from jax.experimental.pallas import tpu as pltpu
from jax.sharding import Mesh
from jax.sharding import PartitionSpec as P

SSM_HEADS = 128
HEAD_P = 64
STATE = 128
HEAD_DIM = 128
PLACES = 64
LANES = 128
GROUP = 16
CTX = ("x", "y", "core")
HIGH = lax.Precision.HIGHEST
F32 = jnp.float32
BF16 = jnp.bfloat16
VMEM_LIMIT = 48 * 1024 * 1024


def dot(a, b, ca, cb, precision=None):
    return lax.dot_general(
        a, b, (((ca,), (cb,)), ((), ())), precision=precision, preferred_element_type=F32
    )


def head_expansion(heads, width):
    row = lax.broadcasted_iota(jnp.int32, (heads, width), 0)
    col = lax.broadcasted_iota(jnp.int32, (heads, width), 1)
    return (col // HEAD_P == row).astype(F32)


def lower_mask(rows):
    t = lax.broadcasted_iota(jnp.int32, (rows, rows), 0)
    s = lax.broadcasted_iota(jnp.int32, (rows, rows), 1)
    return t >= s


def fetch_all(pairs, sems):
    copies = [pltpu.make_async_copy(a, b, sems.at[i]) for i, (a, b) in enumerate(pairs)]
    for copy in copies:
        copy.start()
    return copies


def pack_kernel(key_hbm, value_hbm, out_ref, sems):
    halves = (out_ref.at[:, 0:HEAD_DIM], out_ref.at[:, HEAD_DIM : 2 * HEAD_DIM])
    for copy in fetch_all([(key_hbm, halves[0]), (value_hbm, halves[1])], sems):
        copy.wait()


def state_kernel(decay_hbm, x_hbm, write_hbm, out_ref, decay_ref, x_ref, write_ref, sems):
    copies = fetch_all([(decay_hbm, decay_ref), (x_hbm, x_ref), (write_hbm, write_ref)], sems)
    copies[0].wait()
    rows, width = x_ref.shape
    heads = decay_ref.shape[0]
    share = width // PLACES
    decay = decay_ref[...]
    later = (~lower_mask(rows)).astype(F32)
    tail = jnp.exp(dot(later, decay, 1, 1, HIGH))
    tail = dot(tail, head_expansion(heads, width), 1, 0, HIGH)
    total = dot(decay, jnp.ones((rows, LANES), F32), 1, 0, HIGH)
    high = total.astype(BF16).astype(F32)
    middle = (total - high).astype(BF16).astype(F32)
    low = (total - high - middle).astype(BF16).astype(F32)
    row = lax.broadcasted_iota(jnp.int32, (heads, 8, LANES), 1)
    pieces = jnp.where(
        row == 0,
        high[:, None, :],
        jnp.where(row == 1, middle[:, None, :], jnp.where(row == 2, low[:, None, :], 0.0)),
    )
    pieces = jnp.broadcast_to(pieces[:, None], (heads, PLACES // heads, 8, LANES))
    out_ref[:, share : share + 8, :] = pieces.reshape(PLACES, 8, LANES).astype(BF16)
    copies[1].wait()
    copies[2].wait()
    scaled = (x_ref[...].astype(F32) * tail).astype(BF16)
    state = dot(scaled, write_ref[...], 0, 0)
    out_ref[:, 0:share, :] = state.reshape(PLACES, share, STATE).astype(BF16)


def fold_kernel(parts_ref, out_ref):
    places, deep, lanes = parts_ref.shape
    share = deep - 8
    state = jnp.zeros((share, lanes), F32)
    for i in range(places):
        out_ref[i] = state.astype(BF16)
        if i + 1 < places:
            part = parts_ref[i].astype(F32)
            total = part[share : share + 1] + part[share + 1 : share + 2]
            total = total + part[share + 2 : share + 3]
            state = state * jnp.exp(total) + part[0:share]


def local_kernel(
    decay_hbm,
    read_hbm,
    write_hbm,
    x_hbm,
    gate_hbm,
    skip_hbm,
    held_ref,
    grown_ref,
    skip_ref,
    decay_ref,
    read_ref,
    write_ref,
    x_ref,
    gate_ref,
    sems,
):
    copies = fetch_all(
        [
            (decay_hbm, decay_ref),
            (read_hbm, read_ref),
            (write_hbm, write_ref),
            (x_hbm, x_ref),
            (gate_hbm, gate_ref),
            (skip_hbm, skip_ref),
        ],
        sems,
    )
    copies[0].wait()
    rows, width = x_ref.shape
    heads = decay_ref.shape[0]
    mask = lower_mask(rows)
    lower = mask.astype(F32)
    decay = decay_ref[...]
    cum = dot(lower, decay, 1, 1, HIGH)
    cum_heads = dot(decay, lower, 1, 1, HIGH)
    expansion = head_expansion(heads, width)
    grown = dot(jnp.exp(cum), expansion, 1, 0, HIGH)
    copies[5].wait()
    skip = dot(skip_ref[...], expansion, 1, 0, HIGH)
    copies[1].wait()
    copies[2].wait()
    gain = dot(read_ref[...], write_ref[...], 1, 1)
    copies[3].wait()
    copies[4].wait()
    lane = lax.broadcasted_iota(jnp.int32, (rows, LANES), 1)
    for pair in range(width // LANES):
        cols = slice(pair * LANES, (pair + 1) * LANES)
        x = x_ref[:, cols]
        found = []
        for h in (2 * pair, 2 * pair + 1):
            gap = cum[:, h : h + 1] - cum_heads[h : h + 1, :]
            mix = gain * jnp.exp(jnp.where(mask, gap, -1e30))
            found.append(dot(mix.astype(BF16), x, 1, 0))
        mixed = jnp.where(lane < HEAD_P, found[0], found[1]) + skip[:, cols] * x.astype(F32)
        gate = gate_ref[:, cols].astype(F32)
        gate = gate / (1.0 + jnp.exp(-gate))
        held_ref[:, cols] = mixed * gate
        grown_ref[:, cols] = grown[:, cols] * gate


def carry_kernel(read_hbm, start_ref, held_ref, grown_ref, gated_ref, square_ref, read_ref, sem):
    copies = fetch_all([(read_hbm, read_ref)], sem)
    copies[0].wait()
    rows, width = held_ref.shape
    total = jnp.zeros((rows, LANES), F32)
    for pair in range(width // LANES):
        cols = slice(pair * LANES, (pair + 1) * LANES)
        carry = dot(read_ref[...], start_ref[cols], 1, 1)
        gated = held_ref[:, cols] + carry * grown_ref[:, cols]
        gated_ref[:, cols] = gated
        total = total + gated * gated
    square_ref[:, 0, :] = dot(jnp.ones((8, LANES), F32), total, 1, 1, HIGH)


def norm_kernel(gated_ref, square_ref, gain_ref, out_ref):
    total = dot(square_ref[:, 0, :], jnp.ones((square_ref.shape[0], LANES), F32), 0, 0, HIGH)
    scale = lax.rsqrt(total / (SSM_HEADS * HEAD_P) + 1e-05)
    for c in range(0, out_ref.shape[1], LANES):
        cols = slice(c, c + LANES)
        out_ref[:, cols] = (gated_ref[:, cols] * scale * gain_ref[:, cols]).astype(BF16)


def attention_kernel(place_ref, query_hbm, kv_ref, out_ref, query_ref, kv, top, acc, sems):
    rows = out_ref.shape[0]
    sets = out_ref.shape[1] // HEAD_DIM
    stack = 2 * rows
    factor = 1.4426950408889634 / HEAD_DIM**0.5
    place = place_ref[0]
    last = place // GROUP
    keys_at_once = GROUP * rows

    def fetch(c):
        first = pl.multiple_of((last - c) * rows, rows)
        return pltpu.make_async_copy(kv_ref.at[:, pl.ds(first, rows)], kv.at[c], sems.at[c])

    copies = fetch_all(
        [
            (
                query_hbm.at[:, pl.ds(j * HEAD_DIM, HEAD_DIM)],
                query_ref.at[pl.ds(j * rows, rows)],
            )
            for j in range(sets)
        ],
        sems.at[pl.ds(sems.shape[0] - sets, sets)],
    )

    @pl.loop(0, last + 1)
    def _(c):
        fetch(c).start()

    top[...] = jnp.full(top.shape, -1e30, F32)
    acc[...] = jnp.zeros(acc.shape, F32)
    for copy in copies:
        copy.wait()

    def step(c, diagonal):
        fetch(c).wait()
        block = kv[c].reshape(keys_at_once, 2 * HEAD_DIM)
        keys = block[:, 0:HEAD_DIM]
        values = jnp.concatenate(
            [block[:, HEAD_DIM : 2 * HEAD_DIM], jnp.ones((keys_at_once, LANES), BF16)], axis=1
        )
        if diagonal:
            t = lax.broadcasted_iota(jnp.int32, (rows, keys_at_once), 0) + place * rows
            s = lax.broadcasted_iota(jnp.int32, (rows, keys_at_once), 1) + c * keys_at_once
            visible = jnp.concatenate([s <= t] * (stack // rows), axis=0)

        def scores_of(g):
            scores = dot(query_ref[g * stack : (g + 1) * stack], keys, 1, 1)
            return jnp.where(visible, scores, -1e30) if diagonal else scores

        ahead = scores_of(0)
        for g in range(sets * rows // stack):
            here = slice(g * stack, (g + 1) * stack)
            scores = ahead
            if (g + 1) * stack < sets * rows:
                ahead = scores_of(g + 1)
            old = top[here]
            new = jnp.maximum(old, jnp.max(scores, axis=1, keepdims=True))
            weights = jnp.exp2(scores * factor - new[:, 0:1] * factor).astype(BF16)
            shrink = jnp.exp2((old - new) * factor)
            shrink = jnp.concatenate([shrink, shrink], axis=1)
            acc[here] = acc[here] * shrink + dot(weights, values, 1, 0)
            top[here] = new

    @pl.loop(0, last)
    def _(c):
        step(c, False)

    step(last, True)
    for j in range(sets):
        here = slice(j * rows, (j + 1) * rows)
        out_ref[:, j * HEAD_DIM : (j + 1) * HEAD_DIM] = (
            acc[here, 0:HEAD_DIM] / acc[here, HEAD_DIM : 2 * HEAD_DIM]
        ).astype(BF16)


def vmem_call(kernel, outs, name, flops, moved, **more):
    return pl.pallas_call(
        kernel,
        out_shape=outs,
        name=name,
        compiler_params=pltpu.CompilerParams(vmem_limit_bytes=VMEM_LIMIT),
        cost_estimate=pl.CostEstimate(flops=flops, bytes_accessed=moved, transcendentals=0),
        **more,
    )


def body(
    ssm_input,
    gate_input,
    write_proj,
    read_proj,
    log_decay,
    skip_gain,
    norm_gain,
    query_rows,
    key_rows,
    value_rows,
):
    rows, width = ssm_input.shape
    heads = log_decay.shape[1]
    share = width // PLACES
    place = lax.axis_index(CTX).astype(jnp.int32).reshape(1)
    in_vmem = pl.BlockSpec(memory_space=pltpu.VMEM)
    anywhere = pl.BlockSpec(memory_space=pltpu.HBM)
    x_scratch = pltpu.VMEM((rows, width), BF16)
    decay_scratch = pltpu.VMEM((heads, rows), F32)
    side_scratch = pltpu.VMEM((rows, STATE), BF16)

    key_rows, value_rows, ssm_input, gate_input, write_proj, read_proj, query_rows = (
        pltpu.with_memory_space_constraint(a, pltpu.HBM)
        for a in (
            key_rows, value_rows, ssm_input, gate_input, write_proj, read_proj, query_rows
        )
    )
    decay = pltpu.with_memory_space_constraint(log_decay.T, pltpu.HBM)
    skip_row = pltpu.with_memory_space_constraint(skip_gain[None], pltpu.HBM)

    own = vmem_call(
        pack_kernel,
        jax.ShapeDtypeStruct((rows, 2 * HEAD_DIM), BF16),
        "pack",
        0,
        8 * rows * HEAD_DIM,
        in_specs=[anywhere] * 2,
        scratch_shapes=[pltpu.SemaphoreType.DMA((2,))],
    )(key_rows, value_rows)
    columns = PLACES // GROUP
    held = [own] + [
        lax.ppermute(own, "x", [(i, i + k) for i in range(columns - k)]) for k in range(1, columns)
    ]
    parts = vmem_call(
        state_kernel,
        jax.ShapeDtypeStruct((PLACES, share + 8, STATE), BF16),
        "device_state",
        2 * rows * width * STATE,
        2 * rows * width,
        in_specs=[anywhere] * 3,
        scratch_shapes=[decay_scratch, x_scratch, side_scratch, pltpu.SemaphoreType.DMA((3,))],
    )(decay, ssm_input, write_proj)
    mixed, grown = vmem_call(
        local_kernel,
        (jax.ShapeDtypeStruct((rows, width), F32),) * 2,
        "local",
        4 * rows * rows * width,
        12 * rows * width,
        in_specs=[anywhere] * 6,
        scratch_shapes=[pltpu.VMEM((1, heads), F32), decay_scratch]
        + [side_scratch] * 2
        + [x_scratch] * 2
        + [pltpu.SemaphoreType.DMA((6,))],
    )(decay, read_proj, write_proj, ssm_input, gate_input, skip_row)
    parts, mixed, grown, place, *held = lax.optimization_barrier(
        (parts, mixed, grown, place, *held)
    )
    kv = lax.all_gather(jnp.concatenate(held, axis=0), ("y", "core"), axis=0)
    parts = lax.all_to_all(parts, CTX, 0, 0, tiled=True)
    starts = vmem_call(
        fold_kernel,
        jax.ShapeDtypeStruct((PLACES, share, STATE), BF16),
        "state_fold",
        2 * width * STATE,
        4 * width * STATE,
    )(parts)
    starts = lax.all_to_all(starts, CTX, 0, 0, tiled=True)
    gated, square = vmem_call(
        carry_kernel,
        (
            jax.ShapeDtypeStruct((rows, width), F32),
            jax.ShapeDtypeStruct((8, 1, rows), F32),
        ),
        "carry",
        2 * rows * width * STATE,
        12 * rows * width,
        in_specs=[anywhere] + [in_vmem] * 3,
        scratch_shapes=[side_scratch, pltpu.SemaphoreType.DMA((1,))],
    )(read_proj, starts.reshape(width, STATE), mixed, grown)
    square, query_rows = lax.optimization_barrier((square, query_rows))
    square = lax.all_to_all(square, "heads", 0, 0, tiled=True)
    attn_out = vmem_call(
        attention_kernel,
        jax.ShapeDtypeStruct(query_rows.shape, BF16),
        "attention",
        2 * rows * 4 * PLACES * rows * 2 * HEAD_DIM,
        2 * PLACES * rows * 2 * HEAD_DIM,
        in_specs=[pl.BlockSpec(memory_space=pltpu.SMEM), anywhere, anywhere],
        scratch_shapes=[
            pltpu.VMEM((4 * rows, HEAD_DIM), BF16),
            pltpu.VMEM((columns, GROUP, rows, 2 * HEAD_DIM), BF16),
            pltpu.VMEM((4 * rows, LANES), F32),
            pltpu.VMEM((4 * rows, 2 * HEAD_DIM), F32),
            pltpu.SemaphoreType.DMA((columns + 4,)),
        ],
    )(place, query_rows, kv)
    attn_out, square = lax.optimization_barrier((attn_out, square))
    ssm_out = vmem_call(
        norm_kernel,
        jax.ShapeDtypeStruct((rows, width), BF16),
        "norm",
        4 * rows * width,
        6 * rows * width,
    )(gated, square, norm_gain[None])
    return (ssm_out, attn_out)


def solution(mesh):
    fine = Mesh(mesh.devices.reshape(4, 8, 2, 8), CTX + ("heads",))
    split = P(CTX, "heads")
    in_specs = (
        split,
        split,
        P(CTX, None),
        P(CTX, None),
        split,
        P("heads"),
        P("heads"),
        split,
        split,
        split,
    )
    return jax.shard_map(
        body, mesh=fine, in_specs=in_specs, out_specs=(split, split), check_vma=False
    )
```

```python
import jax
import jax.numpy as jnp
from jax import lax
from jax.experimental import pallas as pl
from jax.experimental.pallas import tpu as pltpu
from jax.sharding import Mesh
from jax.sharding import PartitionSpec as P

SSM_HEADS = 128
HEAD_P = 64
STATE = 128
HEAD_DIM = 128
PLACES = 64
LANES = 128
GROUP = 16
CTX = ("x", "y", "core")
HIGH = lax.Precision.HIGHEST
F32 = jnp.float32
BF16 = jnp.bfloat16
VMEM_LIMIT = 48 * 1024 * 1024


def dot(a, b, ca, cb, precision=None):
    return lax.dot_general(
        a, b, (((ca,), (cb,)), ((), ())), precision=precision, preferred_element_type=F32
    )


def head_expansion(heads, width):
    row = lax.broadcasted_iota(jnp.int32, (heads, width), 0)
    col = lax.broadcasted_iota(jnp.int32, (heads, width), 1)
    return (col // HEAD_P == row).astype(F32)


def lower_mask(rows):
    t = lax.broadcasted_iota(jnp.int32, (rows, rows), 0)
    s = lax.broadcasted_iota(jnp.int32, (rows, rows), 1)
    return t >= s


def fetch_all(pairs, sems):
    copies = [pltpu.make_async_copy(a, b, sems.at[i]) for i, (a, b) in enumerate(pairs)]
    for copy in copies:
        copy.start()
    return copies


def pack_kernel(key_hbm, value_hbm, out_ref, sems):
    halves = (out_ref.at[:, 0:HEAD_DIM], out_ref.at[:, HEAD_DIM : 2 * HEAD_DIM])
    for copy in fetch_all([(key_hbm, halves[0]), (value_hbm, halves[1])], sems):
        copy.wait()


def state_kernel(decay_hbm, x_hbm, write_hbm, out_ref, decay_ref, x_ref, write_ref, sems):
    copies = fetch_all([(decay_hbm, decay_ref), (x_hbm, x_ref), (write_hbm, write_ref)], sems)
    copies[0].wait()
    rows, width = x_ref.shape
    heads = decay_ref.shape[0]
    share = width // PLACES
    decay = decay_ref[...]
    later = (~lower_mask(rows)).astype(F32)
    tail = jnp.exp(dot(later, decay, 1, 1, HIGH))
    tail = dot(tail, head_expansion(heads, width), 1, 0, HIGH)
    total = dot(decay, jnp.ones((rows, LANES), F32), 1, 0, HIGH)
    high = total.astype(BF16).astype(F32)
    middle = (total - high).astype(BF16).astype(F32)
    low = (total - high - middle).astype(BF16).astype(F32)
    row = lax.broadcasted_iota(jnp.int32, (heads, 8, LANES), 1)
    pieces = jnp.where(
        row == 0,
        high[:, None, :],
        jnp.where(row == 1, middle[:, None, :], jnp.where(row == 2, low[:, None, :], 0.0)),
    )
    pieces = jnp.broadcast_to(pieces[:, None], (heads, PLACES // heads, 8, LANES))
    out_ref[:, share : share + 8, :] = pieces.reshape(PLACES, 8, LANES).astype(BF16)
    copies[1].wait()
    copies[2].wait()
    scaled = (x_ref[...].astype(F32) * tail).astype(BF16)
    state = dot(scaled, write_ref[...], 0, 0)
    out_ref[:, 0:share, :] = state.reshape(PLACES, share, STATE).astype(BF16)


def fold_kernel(parts_ref, out_ref):
    places, deep, lanes = parts_ref.shape
    share = deep - 8
    state = jnp.zeros((share, lanes), F32)
    for i in range(places):
        out_ref[i] = state.astype(BF16)
        if i + 1 < places:
            part = parts_ref[i].astype(F32)
            total = part[share : share + 1] + part[share + 1 : share + 2]
            total = total + part[share + 2 : share + 3]
            state = state * jnp.exp(total) + part[0:share]


def local_kernel(
    decay_hbm,
    read_hbm,
    write_hbm,
    x_hbm,
    gate_hbm,
    skip_hbm,
    held_ref,
    grown_ref,
    kept_ref,
    skip_ref,
    decay_ref,
    read_ref,
    write_ref,
    x_ref,
    gate_ref,
    sems,
):
    copies = fetch_all(
        [
            (decay_hbm, decay_ref),
            (read_hbm, read_ref),
            (write_hbm, write_ref),
            (x_hbm, x_ref),
            (gate_hbm, gate_ref),
            (skip_hbm, skip_ref),
        ],
        sems,
    )
    copies[0].wait()
    rows, width = x_ref.shape
    heads = decay_ref.shape[0]
    mask = lower_mask(rows)
    lower = mask.astype(F32)
    decay = decay_ref[...]
    cum = dot(lower, decay, 1, 1, HIGH)
    cum_heads = dot(decay, lower, 1, 1, HIGH)
    expansion = head_expansion(heads, width)
    grown = dot(jnp.exp(cum), expansion, 1, 0, HIGH)
    copies[5].wait()
    skip = dot(skip_ref[...], expansion, 1, 0, HIGH)
    copies[1].wait()
    copies[2].wait()
    kept_ref[...] = read_ref[...]
    gain = dot(read_ref[...], write_ref[...], 1, 1)
    copies[3].wait()
    copies[4].wait()
    lane = lax.broadcasted_iota(jnp.int32, (rows, LANES), 1)
    for pair in range(width // LANES):
        cols = slice(pair * LANES, (pair + 1) * LANES)
        x = x_ref[:, cols]
        found = []
        for h in (2 * pair, 2 * pair + 1):
            gap = cum[:, h : h + 1] - cum_heads[h : h + 1, :]
            mix = gain * jnp.exp(jnp.where(mask, gap, -1e30))
            found.append(dot(mix.astype(BF16), x, 1, 0))
        mixed = jnp.where(lane < HEAD_P, found[0], found[1]) + skip[:, cols] * x.astype(F32)
        gate = gate_ref[:, cols].astype(F32)
        gate = gate / (1.0 + jnp.exp(-gate))
        held_ref[:, cols] = mixed * gate
        grown_ref[:, cols] = grown[:, cols] * gate


def carry_kernel(read_ref, start_ref, held_ref, grown_ref, gated_ref, square_ref):
    rows, width = held_ref.shape
    total = jnp.zeros((rows, LANES), F32)
    for pair in range(width // LANES):
        cols = slice(pair * LANES, (pair + 1) * LANES)
        carry = dot(read_ref[...], start_ref[cols], 1, 1)
        gated = held_ref[:, cols] + carry * grown_ref[:, cols]
        gated_ref[:, cols] = gated
        total = total + gated * gated
    square_ref[:, 0, :] = dot(jnp.ones((8, LANES), F32), total, 1, 1, HIGH)


def norm_kernel(gated_ref, square_ref, gain_ref, out_ref):
    total = dot(square_ref[:, 0, :], jnp.ones((square_ref.shape[0], LANES), F32), 0, 0, HIGH)
    scale = lax.rsqrt(total / (SSM_HEADS * HEAD_P) + 1e-05)
    for c in range(0, out_ref.shape[1], LANES):
        cols = slice(c, c + LANES)
        out_ref[:, cols] = (gated_ref[:, cols] * scale * gain_ref[:, cols]).astype(BF16)


def attention_kernel(place_ref, query_hbm, kv_ref, out_ref, query_ref, kv, top, acc, sems):
    rows = out_ref.shape[0]
    sets = out_ref.shape[1] // HEAD_DIM
    stacked = sets * rows
    members = kv.shape[1]
    factor = 1.4426950408889634 / HEAD_DIM**0.5
    place = place_ref[0]
    last = place // members

    def fetch(c):
        first = pl.multiple_of((last - c) * rows, rows)
        return pltpu.make_async_copy(kv_ref.at[:, pl.ds(first, rows)], kv.at[c], sems.at[c])

    copies = fetch_all(
        [
            (
                query_hbm.at[:, pl.ds(j * HEAD_DIM, HEAD_DIM)],
                query_ref.at[pl.ds(j * rows, rows)],
            )
            for j in range(sets)
        ],
        sems.at[pl.ds(sems.shape[0] - sets, sets)],
    )
    fetch(last).start()

    @pl.loop(0, last)
    def _(c):
        fetch(c).start()

    def load(c, first, count):
        block = kv[c, first : first + count].reshape(count * rows, 2 * HEAD_DIM)
        ones = jnp.ones((count * rows, LANES), BF16)
        return block[:, 0:HEAD_DIM], jnp.concatenate([block[:, HEAD_DIM:], ones], axis=1)

    def weigh(scores, peak):
        return jnp.exp2(scores * factor - peak * factor).astype(BF16)

    def exact_step(c, diagonal):
        keys, values = load(c, 0, members)
        stack = 2 * rows
        if diagonal:
            count = members * rows
            t = lax.broadcasted_iota(jnp.int32, (rows, count), 0) + place * rows
            s = lax.broadcasted_iota(jnp.int32, (rows, count), 1) + c * count
            visible = jnp.concatenate([s <= t] * (stack // rows), axis=0)

        def scores_of(g):
            scores = dot(query_ref[g * stack : (g + 1) * stack], keys, 1, 1)
            return jnp.where(visible, scores, -1e30) if diagonal else scores

        ahead = scores_of(0)
        for g in range(stacked // stack):
            here = slice(g * stack, (g + 1) * stack)
            scores = ahead
            if (g + 1) * stack < stacked:
                ahead = scores_of(g + 1)
            peak = jnp.max(scores, axis=1, keepdims=True)
            if diagonal:
                acc[here] = dot(weigh(scores, peak), values, 1, 0)
                top[here] = jnp.broadcast_to(peak, (stack, LANES))
            else:
                old = top[here]
                new = jnp.maximum(old, peak)
                shrink = jnp.exp2((old - new) * factor)
                shrink = jnp.concatenate([shrink, shrink], axis=1)
                acc[here] = acc[here] * shrink + dot(
                    weigh(scores, new[:, 0:1]), values, 1, 0
                )
                top[here] = new

    for copy in copies:
        copy.wait()
    fetch(last).wait()
    exact_step(last, True)

    @pl.loop(0, last)
    def _(c):
        fetch(c).wait()
        exact_step(c, False)

    for j in range(sets):
        here = slice(j * rows, (j + 1) * rows)
        out_ref[:, j * HEAD_DIM : (j + 1) * HEAD_DIM] = (
            acc[here, 0:HEAD_DIM] / acc[here, HEAD_DIM : 2 * HEAD_DIM]
        ).astype(BF16)


def vmem_call(kernel, outs, name, flops, moved, **more):
    return pl.pallas_call(
        kernel,
        out_shape=outs,
        name=name,
        compiler_params=pltpu.CompilerParams(vmem_limit_bytes=VMEM_LIMIT),
        cost_estimate=pl.CostEstimate(flops=flops, bytes_accessed=moved, transcendentals=0),
        **more,
    )


def body(
    ssm_input,
    gate_input,
    write_proj,
    read_proj,
    log_decay,
    skip_gain,
    norm_gain,
    query_rows,
    key_rows,
    value_rows,
):
    rows, width = ssm_input.shape
    heads = log_decay.shape[1]
    share = width // PLACES
    place = lax.axis_index(CTX).astype(jnp.int32).reshape(1)
    in_vmem = pl.BlockSpec(memory_space=pltpu.VMEM)
    anywhere = pl.BlockSpec(memory_space=pltpu.HBM)
    x_scratch = pltpu.VMEM((rows, width), BF16)
    decay_scratch = pltpu.VMEM((heads, rows), F32)
    side_scratch = pltpu.VMEM((rows, STATE), BF16)

    key_rows, value_rows, ssm_input, gate_input, write_proj, read_proj, query_rows = (
        pltpu.with_memory_space_constraint(a, pltpu.HBM)
        for a in (
            key_rows, value_rows, ssm_input, gate_input, write_proj, read_proj, query_rows
        )
    )
    decay = pltpu.with_memory_space_constraint(log_decay.T, pltpu.HBM)
    skip_row = pltpu.with_memory_space_constraint(skip_gain[None], pltpu.HBM)

    own = vmem_call(
        pack_kernel,
        jax.ShapeDtypeStruct((rows, 2 * HEAD_DIM), BF16),
        "pack",
        0,
        8 * rows * HEAD_DIM,
        in_specs=[anywhere] * 2,
        scratch_shapes=[pltpu.SemaphoreType.DMA((2,))],
    )(key_rows, value_rows)
    columns = PLACES // GROUP
    held = [own] + [
        lax.ppermute(own, "x", [(i, i + k) for i in range(columns - k)]) for k in range(1, columns)
    ]
    parts = vmem_call(
        state_kernel,
        jax.ShapeDtypeStruct((PLACES, share + 8, STATE), BF16),
        "device_state",
        2 * rows * width * STATE,
        2 * rows * width,
        in_specs=[anywhere] * 3,
        scratch_shapes=[decay_scratch, x_scratch, side_scratch, pltpu.SemaphoreType.DMA((3,))],
    )(decay, ssm_input, write_proj)
    mixed, grown, kept = vmem_call(
        local_kernel,
        (
            jax.ShapeDtypeStruct((rows, width), F32),
            jax.ShapeDtypeStruct((rows, width), F32),
            jax.ShapeDtypeStruct((rows, STATE), BF16),
        ),
        "local",
        4 * rows * rows * width,
        12 * rows * width,
        in_specs=[anywhere] * 6,
        scratch_shapes=[pltpu.VMEM((1, heads), F32), decay_scratch]
        + [side_scratch] * 2
        + [x_scratch] * 2
        + [pltpu.SemaphoreType.DMA((6,))],
    )(decay, read_proj, write_proj, ssm_input, gate_input, skip_row)
    parts, mixed, grown, kept, place, *held = lax.optimization_barrier(
        (parts, mixed, grown, kept, place, *held)
    )
    kv = lax.all_gather(jnp.concatenate(held, axis=0), ("y", "core"), axis=0)
    parts = lax.all_to_all(parts, CTX, 0, 0, tiled=True)
    starts = vmem_call(
        fold_kernel,
        jax.ShapeDtypeStruct((PLACES, share, STATE), BF16),
        "state_fold",
        2 * width * STATE,
        4 * width * STATE,
    )(parts)
    starts = lax.all_to_all(starts, CTX, 0, 0, tiled=True)
    gated, square = vmem_call(
        carry_kernel,
        (
            jax.ShapeDtypeStruct((rows, width), F32),
            jax.ShapeDtypeStruct((8, 1, rows), F32),
        ),
        "carry",
        2 * rows * width * STATE,
        12 * rows * width,
    )(kept, starts.reshape(width, STATE), mixed, grown)
    square, query_rows = lax.optimization_barrier((square, query_rows))
    square = lax.all_to_all(square, "heads", 0, 0, tiled=True)
    attn_out = vmem_call(
        attention_kernel,
        jax.ShapeDtypeStruct(query_rows.shape, BF16),
        "attention",
        2 * rows * 4 * PLACES * rows * 2 * HEAD_DIM,
        2 * PLACES * rows * 2 * HEAD_DIM,
        in_specs=[pl.BlockSpec(memory_space=pltpu.SMEM), anywhere, anywhere],
        scratch_shapes=[
            pltpu.VMEM((4 * rows, HEAD_DIM), BF16),
            pltpu.VMEM((columns, GROUP, rows, 2 * HEAD_DIM), BF16),
            pltpu.VMEM((4 * rows, LANES), F32),
            pltpu.VMEM((4 * rows, 2 * HEAD_DIM), F32),
            pltpu.SemaphoreType.DMA((columns + 4,)),
        ],
    )(place, query_rows, kv)
    attn_out, square = lax.optimization_barrier((attn_out, square))
    ssm_out = vmem_call(
        norm_kernel,
        jax.ShapeDtypeStruct((rows, width), BF16),
        "norm",
        4 * rows * width,
        6 * rows * width,
    )(gated, square, norm_gain[None])
    return (ssm_out, attn_out)


def solution(mesh):
    fine = Mesh(mesh.devices.reshape(4, 8, 2, 8), CTX + ("heads",))
    split = P(CTX, "heads")
    in_specs = (
        split,
        split,
        P(CTX, None),
        P(CTX, None),
        split,
        P("heads"),
        P("heads"),
        split,
        split,
        split,
    )
    return jax.shard_map(
        body, mesh=fine, in_specs=in_specs, out_specs=(split, split), check_vma=False
    )
```
